256 devices in a mesh: blk: 8 (over x, core), sub: 32 (over z, y).
Axes of the slice: x: 4, y: 4, z: 8, core: 2. Of those that a mesh axis runs over, the one named last changes fastest.
Arguments:
- user_factors: float32 [262144, 1024], P(('blk', 'sub')), may hold values from -6 to 6
- item_factors: bfloat16 [2048, 1024], P(('blk', 'sub')), may hold values from -6 to 6
- ratings: bfloat16 [262144, 1024], P(('blk', 'sub')), may hold values from -6 to 6
- presence: int32 [2048, 8, 2], P(('blk', 'sub')), may hold values 0 or 1
- visit_order: int32 [8], replicated, may hold values from 0 to 7, each once
Outputs:
- users_out: float32 [262144, 1024], P(('blk', 'sub'))
- items_out: bfloat16 [2048, 1024], P(('blk', 'sub'))
The draws below stay inside these ranges and needn't reach their ends.
All inputs are finite; a program needn't handle non-finite values. No bound on the sum of `presence` on one device may be relied on, other than what follows from the above.
Results may differ from the reference program's by a relative error of at most 0.017.
Values may be sent and summed in bfloat16 or wider, within the bound.
No kernel may reach another device: no remote copies, remote signals or barrier semaphores. Data moves between devices by JAX's collectives and lax.ppermute only.
A program may use at most 64 MiB of HBM per device.

```python
import math
import jax
import jax.numpy as jnp
from jax import lax

R = 1024
BS = 256
TILE = 128
TICKS = 4
U_DEV = 1024
USERS = 262144
ITEMS = 2048
N_BLK = 8
N_SUB = 32


def draw_user_factors(key, part):
    inner = jax.random.fold_in(key, 11)
    values = jnp.clip(jax.random.normal(inner, (USERS, R), jnp.float32), -6.0, 6.0)
    return values


def draw_item_factors(key, part):
    inner = jax.random.fold_in(key, 23)
    values = jnp.clip(jax.random.normal(inner, (ITEMS, R), jnp.float32), -6.0, 6.0)
    return values.astype(jnp.bfloat16)


def place_ends(values, stream_key, smallest, high):
    shape = values.shape
    index_at = [jax.random.randint(jax.random.fold_in(stream_key, axis), (), 0, shape[axis]) for axis in range(len(shape))]
    values = values.at[tuple(index_at)].set(smallest)
    longest = shape.index(max(shape))
    index_at[longest] = (index_at[longest] + 1) % shape[longest]
    return values.at[tuple(index_at)].set(high)


def block_scale(rng, dims, pieces, smallest, high):
    level = 1.0
    for axis_at, blocks in pieces:
        draws = jax.random.uniform(jax.random.fold_in(jax.random.fold_in(rng, 6), axis_at), (blocks,), jnp.float32, smallest / len(pieces), high / len(pieces))
        level = level * jnp.repeat(jnp.exp(draws), dims[axis_at] // blocks).reshape((-1,) + (1,) * (len(dims) - 1 - axis_at))
    return level


def bell_draw(rng, dims, spread, limit, cuts=(), held_as=jnp.bfloat16):
    array = spread * jax.random.normal(rng, dims, jnp.float32)
    if cuts:
        array = array * block_scale(rng, dims, cuts, -0.22, 0.18)
    return jnp.clip(array, -limit, limit).astype(held_as)


def setup_inputs(seed: int = 0) -> dict:
    key_of = jax.random.split(jax.random.key(seed), 6)
    return {
        "user_factors": draw_user_factors(jax.random.fold_in(key_of[5], 71), 0),
        "item_factors": draw_item_factors(jax.random.fold_in(key_of[5], 71), 0),
        "ratings": bell_draw(key_of[2], (USERS, TICKS * BS), 1.0, 6.0, ((0, 256),)),
        "presence": place_ends((jax.random.randint(key_of[3], (USERS // TILE, N_BLK, BS // TILE), 0, 2) < 1).astype(jnp.int32), jax.random.fold_in(key_of[3], 1), 0, 1),
        "visit_order": jax.random.permutation(key_of[4], N_BLK).astype(jnp.int32),
    }


learn_users = 0.5
decay_weight = 0.05

def reference(user_factors, item_factors, ratings, presence, visit_order):
    scale = R ** (-0.5)
    step_items = 0.9 * R / (math.sqrt(N_SUB * U_DEV) + math.sqrt(R)) ** 2
    tile_users = U_DEV // TILE
    tile_items = BS // TILE
    held = item_factors.reshape(N_BLK, BS, R)
    grouped = user_factors.reshape(N_BLK, N_SUB, U_DEV, R)
    pres_grouped = presence.reshape(N_BLK, N_SUB, tile_users, N_BLK, tile_items)
    rate_grouped = ratings.reshape(N_BLK, N_SUB, U_DEV, TICKS, BS)
    for step_index in range(TICKS):
        idents = jnp.roll(visit_order, step_index).astype(jnp.int32)

        def visit(packed):
            users_now, block_now, pres_now, rate_now, ident = packed
            picked = jnp.take(pres_now, ident, axis=2)
            present = jnp.broadcast_to(picked[:, :, None, :, None], (N_SUB, tile_users, TILE, tile_items, TILE))
            present = present.reshape(N_SUB, U_DEV, BS).astype(jnp.float32)
            users_half = users_now.astype(jnp.bfloat16).astype(jnp.float32)
            block_wide = block_now.astype(jnp.float32)
            predicted = jnp.einsum('sur,ir->sui', users_half, block_wide) * scale
            residual = (present * (predicted - rate_now.astype(jnp.float32))).astype(jnp.bfloat16).astype(jnp.float32)
            user_grad = jnp.einsum('sui,ir->sur', residual, block_wide) * scale
            item_part = (jnp.einsum('sui,sur->sir', residual, users_half) * scale).astype(jnp.bfloat16)
            item_grad = lax.optimization_barrier(jnp.sum(item_part.astype(jnp.float32), axis=0))
            users_next = users_now - learn_users * (user_grad + decay_weight * users_now)
            block_next = (block_wide - step_items * (item_grad + decay_weight * block_wide)).astype(jnp.bfloat16)
            return (users_next, block_next)
        grouped, updated = lax.map(visit, (grouped, held, pres_grouped, rate_grouped[:, :, :, step_index], idents))
        held = jnp.roll(updated, 1, axis=0)
    return (grouped.reshape(USERS, R), held.reshape(ITEMS, R))
```

```python
import math

import jax
import jax.numpy as jnp
from jax import lax
from jax.sharding import Mesh, PartitionSpec as P

R = 1024
BS = 256
TICKS = 4
NZ = 8
NY = 4


learn_users = 0.5
decay_weight = 0.05


def route(size_blk, shift_blk, shift_y):
    pairs = []
    for g in range(size_blk):
        for y in range(NY):
            pairs.append((g * NY + y, ((g + shift_blk) % size_blk) * NY + (y + shift_y) % NY))
    return pairs


def gather_z(rows):
    return lax.all_to_all(jnp.broadcast_to(rows[None], (NZ,) + rows.shape), "z", 0, 0)


def gather_block(rows, shift):
    groups = lax.axis_size("blk")
    y = lax.axis_index("y")
    part = gather_z(rows)
    order = [2, 1, 3, 0]
    got = {}
    for k in order:
        if k == 0 and shift == 0:
            got[k] = part
        else:
            got[k] = lax.ppermute(part, ("blk", "y"), route(groups, shift, k))
    block = jnp.zeros((NZ, NY) + rows.shape, rows.dtype)
    for k in range(NY):
        block = lax.dynamic_update_slice(block, got[k][:, None], (0, jnp.mod(y - k, NY), 0, 0))
    own = lax.dynamic_index_in_dim(got[0], lax.axis_index("z"), 0, keepdims=False)
    return block, own


def reduce_rows(item_part):
    y = lax.axis_index("y")
    groups = lax.axis_size("blk")
    terms = []
    for k in (2, 1, 3):
        chunk = lax.dynamic_index_in_dim(item_part, jnp.mod(y + k, NY), 1, keepdims=False)
        terms.append(lax.ppermute(chunk, ("blk", "y"), route(groups, 0, k)))
    own = lax.dynamic_index_in_dim(item_part, y, 1, keepdims=False)
    total = own.astype(jnp.float32)
    for term in terms:
        total = total + term.astype(jnp.float32)
    spread = lax.all_to_all(total.astype(jnp.bfloat16), "z", 0, 0)
    return jnp.sum(spread.astype(jnp.float32), axis=0)


def on_device(user_factors, item_factors, ratings, presence, visit_order):
    scale = R ** (-0.5)
    group_count = lax.axis_size("blk")
    group = lax.axis_index("blk")
    local_users = user_factors.shape[0]
    group_users = NZ * NY * local_users
    step_items = 0.9 * R / (math.sqrt(group_users) + math.sqrt(R)) ** 2
    tile_users = presence.shape[0]
    tile_items = presence.shape[2]
    users_now = user_factors
    block, own = gather_block(item_factors, 0)
    for step_index in range(TICKS):
        position = jnp.mod(group - step_index, group_count)
        ident = jnp.sum(jnp.where(jnp.arange(group_count) == position, visit_order, 0))
        picked = lax.dynamic_index_in_dim(presence, ident, 1, keepdims=False)
        present = jnp.broadcast_to(
            picked[:, None, :, None],
            (tile_users, local_users // tile_users, tile_items, BS // tile_items),
        )
        present = present.reshape(local_users, BS).astype(jnp.float32)
        users_half = users_now.astype(jnp.bfloat16)
        item_block = block.reshape(BS, R)
        predicted = (
            lax.dot_general(
                users_half, item_block, (((1,), (1,)), ((), ())), preferred_element_type=jnp.float32
            )
            * scale
        )
        targets = ratings[:, step_index * BS : (step_index + 1) * BS].astype(jnp.float32)
        residual = (present * (predicted - targets)).astype(jnp.bfloat16)
        item_part = (
            lax.dot_general(
                residual, users_half, (((0,), (0,)), ((), ())), preferred_element_type=jnp.float32
            )
            * scale
        ).astype(jnp.bfloat16)
        user_grad = jnp.dot(residual, item_block, preferred_element_type=jnp.float32) * scale
        users_now = users_now - learn_users * (user_grad + decay_weight * users_now)
        item_grad = reduce_rows(item_part.reshape(block.shape))
        own_wide = own.astype(jnp.float32)
        updated = (own_wide - step_items * (item_grad + decay_weight * own_wide)).astype(
            jnp.bfloat16
        )
        if step_index < TICKS - 1:
            block, own = gather_block(updated, 1)
        else:
            own = lax.ppermute(updated, ("blk", "y"), route(group_count, 1, 0))
    return (users_now, own)


def solution(mesh):
    axes = ("blk", "z", "y")
    fine = Mesh(mesh.devices.reshape(mesh.shape["blk"], NZ, NY), axes)
    rows = P(axes, None)
    in_specs = (rows, rows, rows, P(axes, None, None), P())
    return jax.shard_map(
        on_device, mesh=fine, in_specs=in_specs, out_specs=(rows, rows), check_vma=False
    )
```

```python
import math

import jax
import jax.numpy as jnp
from jax import lax
from jax.sharding import Mesh, PartitionSpec as P

R = 1024
BS = 256
TICKS = 4
NZ = 8
NY = 4


learn_users = 0.5
decay_weight = 0.05


def moved(value, shift_blk, shift_y):
    groups = lax.axis_size("blk")
    pairs = []
    for g in range(groups):
        for y in range(NY):
            to = ((g + shift_blk) % groups) * NY + (y + shift_y) % NY
            pairs.append((g * NY + y, to))
    return lax.ppermute(value, ("blk", "y"), pairs)


def spread_z(rows):
    return lax.all_to_all(jnp.broadcast_to(rows[None], (NZ,) + rows.shape), "z", 0, 0)


def gather_y(part, shift):
    y = lax.axis_index("y")
    got = {}
    for k in (0, 1, 3, 2):
        got[k] = part if k == 0 and shift == 0 else moved(part, shift, k)
    block = jnp.zeros((NZ, NY) + part.shape[1:], part.dtype)
    for k in (0, 1, 3, 2):
        block = lax.dynamic_update_slice(block, got[k][:, None], (0, jnp.mod(y - k, NY), 0, 0))
    own = lax.dynamic_index_in_dim(got[0], lax.axis_index("z"), 0, keepdims=False)
    return block, own


def reduce_y(item_part, shift):
    y = lax.axis_index("y")
    terms = []
    for k in (1, 3, 2, 0):
        chunk = lax.dynamic_index_in_dim(item_part, jnp.mod(y + k, NY), 1, keepdims=False)
        terms.append(chunk if k == 0 and shift == 0 else moved(chunk, shift, k))
    total = terms[3].astype(jnp.float32)
    for term in terms[:3]:
        total = total + term.astype(jnp.float32)
    return total.astype(jnp.bfloat16)


def masks_of(presence, visit_order, rows):
    groups = lax.axis_size("blk")
    group = lax.axis_index("blk")
    tile_users, _, tile_items = presence.shape
    position = jnp.mod(group - jnp.arange(TICKS), groups)
    at = (position[:, None] == jnp.arange(groups)[None, :])[:, :, None]
    is_block = visit_order[None, :, None] == jnp.arange(groups)[None, None, :]
    chosen = jnp.any(at & is_block, axis=1)
    picked = jnp.sum(jnp.where(chosen[:, None, :, None], presence[None], 0), axis=2)
    picked = picked.astype(jnp.bfloat16)
    wide = jnp.broadcast_to(
        picked[:, :, None, :, None],
        (TICKS, tile_users, rows // tile_users, tile_items, BS // tile_items),
    )
    return wide.reshape(TICKS, rows, BS)


def on_device(user_factors, item_factors, ratings, presence, visit_order):
    scale = R ** (-0.5)
    local_users = user_factors.shape[0]
    group_users = NZ * NY * local_users
    step_items = 0.9 * R / (math.sqrt(group_users) + math.sqrt(R)) ** 2
    users_now = user_factors
    part = spread_z(item_factors)
    masks = masks_of(presence, visit_order, local_users)
    users_half = users_now.astype(jnp.bfloat16)
    part, masks, users_half = lax.optimization_barrier((part, masks, users_half))
    block, own = gather_y(part, 0)
    for step_index in range(TICKS):
        last = step_index == TICKS - 1
        if last:
            own = moved(own, 1, 0)
        item_block = block.reshape(BS, R)
        predicted = (
            lax.dot_general(
                users_half, item_block, (((1,), (1,)), ((), ())), preferred_element_type=jnp.float32
            )
            * scale
        )
        targets = ratings[:, step_index * BS : (step_index + 1) * BS].astype(jnp.float32)
        present = masks[step_index].astype(jnp.float32)
        residual = (present * (predicted - targets)).astype(jnp.bfloat16)
        item_part = (
            lax.dot_general(
                residual, users_half, (((0,), (0,)), ((), ())), preferred_element_type=jnp.float32
            )
            * scale
        ).astype(jnp.bfloat16)
        total = reduce_y(item_part.reshape(block.shape), 1 if last else 0)
        terms = lax.all_to_all(total, "z", 0, 0)
        user_grad = jnp.dot(residual, item_block, preferred_element_type=jnp.float32) * scale
        users_now = users_now - learn_users * (user_grad + decay_weight * users_now)
        if last:
            terms, users_now = lax.optimization_barrier((terms, users_now))
        else:
            users_half = users_now.astype(jnp.bfloat16)
            terms, users_now, users_half = lax.optimization_barrier((terms, users_now, users_half))
        item_grad = jnp.sum(terms.astype(jnp.float32), axis=0)
        own_wide = own.astype(jnp.float32)
        updated = (own_wide - step_items * (item_grad + decay_weight * own_wide)).astype(
            jnp.bfloat16
        )
        if not last:
            block, own = gather_y(spread_z(updated), 1)
    return (users_now, updated)


def solution(mesh):
    axes = ("blk", "z", "y")
    fine = Mesh(mesh.devices.reshape(mesh.shape["blk"], NZ, NY), axes)
    rows = P(axes, None)
    in_specs = (rows, rows, rows, P(axes, None, None), P())
    return jax.shard_map(
        on_device, mesh=fine, in_specs=in_specs, out_specs=(rows, rows), check_vma=False
    )
```

```python
import math

import jax
import jax.numpy as jnp
from jax import lax
from jax.sharding import Mesh, PartitionSpec as P

R = 1024
BS = 256
TICKS = 4
NZ = 8
NY = 4
HALVES = ((2, 3), (1, 0))
ORDER = tuple(k for half in HALVES for k in half)


learn_users = 0.5
decay_weight = 0.05


def moved(value, shift_blk, shift_y):
    groups = lax.axis_size("blk")
    pairs = []
    for g in range(groups):
        for y in range(NY):
            to = ((g + shift_blk) % groups) * NY + (y + shift_y) % NY
            pairs.append((g * NY + y, to))
    return lax.ppermute(value, ("blk", "y"), pairs)


def spread_z(rows):
    return lax.all_to_all(jnp.broadcast_to(rows[None], (NZ,) + rows.shape), "z", 0, 0)


def gather_y(part, shift):
    return {k: part if k == 0 and shift == 0 else moved(part, shift, k) for k in ORDER}


def choose_tiles(presence, visit_order):
    groups = lax.axis_size("blk")
    group = lax.axis_index("blk")
    position = jnp.mod(group - jnp.arange(TICKS), groups)
    at = (position[:, None] == jnp.arange(groups)[None, :])[:, :, None]
    is_block = visit_order[None, :, None] == jnp.arange(groups)[None, None, :]
    chosen = jnp.any(at & is_block, axis=1)
    picked = jnp.sum(jnp.where(chosen[:, None, :, None], presence[None], 0), axis=2)
    return picked.astype(jnp.bfloat16)


def visit_inputs(ratings, tiles, step_index):
    rows = ratings.shape[0]
    tile_users = tiles.shape[1]
    y = lax.axis_index("y")
    column = jnp.arange(BS)
    place, z, r = column // (NZ * 8), column % (NZ * 8) // 8, column % 8
    k = jnp.where(place == 0, ORDER[0], jnp.where(place == 1, ORDER[1], jnp.where(place == 2, ORDER[2], ORDER[3])))
    natural = z * (NY * 8) + jnp.mod(y - k, NY) * 8 + r
    tile_item = natural // (BS // tiles.shape[2])
    pick_row = (jnp.arange(rows)[:, None] // (rows // tile_users) == jnp.arange(tile_users)[None, :])
    wide = jnp.where(tile_item[None, :] == 0, tiles[step_index, :, 0:1], tiles[step_index, :, 1:2])
    mask = jnp.dot(pick_row.astype(jnp.bfloat16), wide, preferred_element_type=jnp.float32)
    to_order = (jnp.arange(BS)[:, None] == natural[None, :]).astype(jnp.bfloat16)
    targets = jnp.dot(
        ratings[:, step_index * BS : (step_index + 1) * BS], to_order, preferred_element_type=jnp.float32
    )
    return mask.astype(jnp.bfloat16), (mask * targets).astype(jnp.bfloat16)


def on_device(user_factors, item_factors, ratings, presence, visit_order):
    scale = R ** (-0.5)
    local_users = user_factors.shape[0]
    group_users = NZ * NY * local_users
    step_items = 0.9 * R / (math.sqrt(group_users) + math.sqrt(R)) ** 2
    width = NZ * 8
    users_now = user_factors
    part = spread_z(item_factors)
    tiles = choose_tiles(presence, visit_order)
    users_half = users_now.astype(jnp.bfloat16)
    part, tiles, users_half = lax.optimization_barrier((part, tiles, users_half))
    chunks = gather_y(part, 0)
    own = item_factors
    for step_index in range(TICKS):
        last = step_index == TICKS - 1
        shift = 1 if last else 0
        sums = []
        residuals = []
        blocks = []
        mask, targets = visit_inputs(ratings, tiles, step_index)
        first = tuple(chunks[k] for k in HALVES[0])
        first, mask, targets = lax.optimization_barrier((first, mask, targets))
        chunks.update(zip(HALVES[0], first))
        for index, half in enumerate(HALVES):
            columns = slice(index * len(half) * width, (index + 1) * len(half) * width)
            items = jnp.concatenate([chunks[k].reshape(width, R) for k in half], axis=0)
            predicted = (
                lax.dot_general(
                    users_half, items, (((1,), (1,)), ((), ())), preferred_element_type=jnp.float32
                )
                * scale
            )
            residual = (
                mask[:, columns].astype(jnp.float32) * predicted
                - targets[:, columns].astype(jnp.float32)
            ).astype(jnp.bfloat16)
            item_part = (
                lax.dot_general(
                    residual, users_half, (((0,), (0,)), ((), ())), preferred_element_type=jnp.float32
                )
                * scale
            ).astype(jnp.bfloat16)
            if index == 0:
                item_part, mask, targets = lax.optimization_barrier((item_part, mask, targets))
            for place, k in enumerate(half):
                piece = item_part[place * width : (place + 1) * width].reshape(NZ, 8, R)
                sums.append(piece if k == 0 and shift == 0 else moved(piece, shift, (-k) % NY))
            residuals.append(residual)
            blocks.append(items)
        if last:
            own = moved(own, 1, 0)
        residual = jnp.concatenate(residuals, axis=1)
        item_block = jnp.concatenate(blocks, axis=0)
        user_grad = jnp.dot(residual, item_block, preferred_element_type=jnp.float32) * scale
        users_now = users_now - learn_users * (user_grad + decay_weight * users_now)
        users_half = users_now.astype(jnp.bfloat16)
        sums, users_now, users_half = lax.optimization_barrier((sums, users_now, users_half))
        total = sums[-1].astype(jnp.float32)
        for term in sums[:-1]:
            total = total + term.astype(jnp.float32)
        terms = lax.all_to_all(total.astype(jnp.bfloat16), "z", 0, 0)
        item_grad = jnp.sum(terms.astype(jnp.float32), axis=0)
        own_wide = own.astype(jnp.float32)
        updated = (own_wide - step_items * (item_grad + decay_weight * own_wide)).astype(
            jnp.bfloat16
        )
        if not last:
            part, tiles = lax.optimization_barrier((spread_z(updated), tiles))
            chunks = gather_y(part, 1)
            own = lax.dynamic_index_in_dim(chunks[0], lax.axis_index("z"), 0, keepdims=False)
    return (users_now, updated)


def solution(mesh):
    axes = ("blk", "z", "y")
    fine = Mesh(mesh.devices.reshape(mesh.shape["blk"], NZ, NY), axes)
    rows = P(axes, None)
    in_specs = (rows, rows, rows, P(axes, None, None), P())
    return jax.shard_map(
        on_device, mesh=fine, in_specs=in_specs, out_specs=(rows, rows), check_vma=False
    )
```

```python
import math

import jax
import jax.numpy as jnp
from jax import lax
from jax.sharding import Mesh, PartitionSpec as P


R = 1024
BS = 256
TICKS = 4
NZ = 8
NY = 4
HALVES = ((3, 2), (1, 0))
ORDER = tuple(k for half in HALVES for k in half)


learn_users = 0.5
decay_weight = 0.05


def moved(value, shift_blk, shift_y):
    groups = lax.axis_size("blk")
    pairs = []
    for g in range(groups):
        for y in range(NY):
            to = ((g + shift_blk) % groups) * NY + (y + shift_y) % NY
            pairs.append((g * NY + y, to))
    return lax.ppermute(value, ("blk", "y"), pairs)


def spread_z(rows):
    return lax.all_to_all(jnp.broadcast_to(rows[None], (NZ,) + rows.shape), "z", 0, 0)


def arriving(part, shift, half):
    return {k: part if k == 0 and shift == 0 else moved(part, shift, k) for k in half}


def choose_tiles(presence, visit_order):
    groups = lax.axis_size("blk")
    group = lax.axis_index("blk")
    position = jnp.mod(group - jnp.arange(TICKS), groups)
    at = (position[:, None] == jnp.arange(groups)[None, :])[:, :, None]
    is_block = visit_order[None, :, None] == jnp.arange(groups)[None, None, :]
    chosen = jnp.any(at & is_block, axis=1)
    picked = jnp.sum(jnp.where(chosen[:, None, :, None], presence[None], 0), axis=2)
    return picked.astype(jnp.bfloat16)


def visit_inputs(ratings, tiles, step_index):
    rows = ratings.shape[0]
    tile_users = tiles.shape[1]
    y = lax.axis_index("y")
    column = jnp.arange(BS)
    place, z, r = column // (NZ * 8), column % (NZ * 8) // 8, column % 8
    k = jnp.where(place == 0, ORDER[0], jnp.where(place == 1, ORDER[1], jnp.where(place == 2, ORDER[2], ORDER[3])))
    natural = z * (NY * 8) + jnp.mod(y - k, NY) * 8 + r
    tile_item = natural // (BS // tiles.shape[2])
    pick_row = (jnp.arange(rows)[:, None] // (rows // tile_users) == jnp.arange(tile_users)[None, :])
    wide = jnp.where(tile_item[None, :] == 0, tiles[step_index, :, 0:1], tiles[step_index, :, 1:2])
    mask = jnp.dot(pick_row.astype(jnp.bfloat16), wide, preferred_element_type=jnp.float32)
    to_order = (jnp.arange(BS)[:, None] == natural[None, :]).astype(jnp.bfloat16)
    targets = jnp.dot(
        ratings[:, step_index * BS : (step_index + 1) * BS], to_order, preferred_element_type=jnp.float32
    )
    return mask.astype(jnp.bfloat16), (mask * targets).astype(jnp.bfloat16)


def on_device(user_factors, item_factors, ratings, presence, visit_order):
    scale = R ** (-0.5)
    local_users = user_factors.shape[0]
    group_users = NZ * NY * local_users
    step_items = 0.9 * R / (math.sqrt(group_users) + math.sqrt(R)) ** 2
    width = NZ * 8
    users_now = user_factors
    part = spread_z(item_factors)
    tiles = choose_tiles(presence, visit_order)
    users_half = users_now.astype(jnp.bfloat16)
    part, tiles, users_half = lax.optimization_barrier((part, tiles, users_half))
    came = 0
    own = item_factors
    for step_index in range(TICKS):
      last = step_index == TICKS - 1
      shift = 1 if last else 0
      sums = []
      residuals = []
      blocks = []
      chunks = arriving(part, came, HALVES[0])
      mask, targets = visit_inputs(ratings, tiles, step_index)
      part, mask, targets = lax.optimization_barrier((part, mask, targets))
      chunks.update(arriving(part, came, HALVES[1]))
      if came:
          own = lax.dynamic_index_in_dim(chunks[0], lax.axis_index("z"), 0, keepdims=False)
      if last:
          own = moved(own, 1, 0)
      for index, half in enumerate(HALVES):
          columns = slice(index * len(half) * width, (index + 1) * len(half) * width)
          items = jnp.concatenate([chunks[k].reshape(width, R) for k in half], axis=0)
          predicted = (
              lax.dot_general(
                  users_half, items, (((1,), (1,)), ((), ())), preferred_element_type=jnp.float32
              )
              * scale
          )
          residual = (
              mask[:, columns].astype(jnp.float32) * predicted
              - targets[:, columns].astype(jnp.float32)
          ).astype(jnp.bfloat16)
          item_part = (
              lax.dot_general(
                  residual, users_half, (((0,), (0,)), ((), ())), preferred_element_type=jnp.float32
              )
              * scale
          ).astype(jnp.bfloat16)
          if index == 0:
              item_part, mask, targets = lax.optimization_barrier((item_part, mask, targets))
          for place, k in enumerate(half):
              piece = item_part[place * width : (place + 1) * width].reshape(NZ, 8, R)
              sums.append(piece if k == 0 and shift == 0 else moved(piece, shift, (-k) % NY))
          residuals.append(residual)
          blocks.append(items)
      residual = jnp.concatenate(residuals, axis=1)
      item_block = jnp.concatenate(blocks, axis=0)
      user_grad = jnp.dot(residual, item_block, preferred_element_type=jnp.float32) * scale
      users_now = users_now - learn_users * (user_grad + decay_weight * users_now)
      users_half = users_now.astype(jnp.bfloat16)
      sums, users_now, users_half, own = lax.optimization_barrier((sums, users_now, users_half, own))
      total = sums[-1].astype(jnp.float32)
      for term in sums[:-1]:
          total = total + term.astype(jnp.float32)
      terms = lax.all_to_all(total.astype(jnp.bfloat16), "z", 0, 0)
      item_grad = jnp.sum(terms.astype(jnp.float32), axis=0)
      own_wide = own.astype(jnp.float32)
      updated = (own_wide - step_items * (item_grad + decay_weight * own_wide)).astype(
          jnp.bfloat16
      )
      if not last:
          part, tiles = lax.optimization_barrier((spread_z(updated), tiles))
          came = 1
    return (users_now, updated)


def solution(mesh):
    axes = ("blk", "z", "y")
    fine = Mesh(mesh.devices.reshape(mesh.shape["blk"], NZ, NY), axes)
    rows = P(axes, None)
    in_specs = (rows, rows, rows, P(axes, None, None), P())
    return jax.shard_map(
        on_device, mesh=fine, in_specs=in_specs, out_specs=(rows, rows), check_vma=False
    )
```
